128 devices in a mesh: row: 8 (over y_hi, z), col: 16 (over x, y_lo, core).
Axes of the slice: x: 4, y: 4 (y_hi: 2, y_lo: 2; y = y_hi * 2 + y_lo), z: 4, core: 2. Of those that a mesh axis runs over, the one named last changes fastest.
Arguments:
- a_panels: float32 [8192, 4096], P('row', 'col'), may hold values from -6 to 6
- b_panels: float32 [4096, 32768], P('row', 'col'), may hold values from -0.1875 to 0.1875
- a_occupancy: int32 [64, 32], P('row', 'col'), may hold values 0 or 1
- b_occupancy: int32 [32, 256], P('row', 'col'), may hold values 0 or 1
- owner_device: int32 [8, 16, 128, 1], P('row', 'col'), may hold values from 0 to 127; in each aligned block of 128 rows (0 to 127, 128 to 255, ..., all dimensions but the last counted through in order) at most 2 rows name the same one
- owner_block: int32 [8, 16, 128], P('row', 'col'), may hold values from 0 to 127
- c_previous: float32 [8, 16, 128, 128, 128], P('row', 'col'), may hold values from -6 to 6
Outputs:
- c_owned: float32 [8, 16, 128, 128, 128], P('row', 'col')
The draws below stay inside these ranges and needn't reach their ends.
Inputs may be any that keep to these rules, and one draw needn't show every extreme that they name: `owner_device`: among the 128 product blocks of one device, at most 2 name the same owner; some owner is named exactly 2 times by one device.
All inputs are finite; a program needn't handle non-finite values. No bound on the sum of `a_occupancy` or of `b_occupancy` on one device may be relied on, other than what follows from the above.
Results may differ from the reference program's by a relative error of at most 0.0003.
Values sent between devices are 32-bit elements; how exact they have to be, the bound alone decides.
A program may use at most 192 MiB of HBM per device.

```python
import math
import jax
import jax.numpy as jnp
import numpy as np
from jax import lax

BLK = 128
P_SIZE = 8
Q = 16
K = 2
TICKS = 4
NBLK = 128
OWN = 128
IMAGES = 2
CAP = 2
N_ROW = 8
N_COL = 16


def touch_ends(drawn, stream_key, least, high):
    longest = drawn.shape.index(max(drawn.shape))
    spots = []
    for shift in (0, 1):
        where = [jax.random.randint(jax.random.fold_in(stream_key, axis), (), 0, length) for axis, length in enumerate(drawn.shape)]
        where[longest] = (where[longest] + shift) % drawn.shape[longest]
        spots.append(tuple(where))
    return drawn.at[spots[0]].set(least).at[spots[1]].set(high)


def steps_of(stream_key, extent, cuts, least, top_value):
    def one(position, parts):
        heights = jax.random.uniform(jax.random.fold_in(jax.random.fold_in(stream_key, 6), position), (parts,), jnp.float32, least / len(cuts), top_value / len(cuts))
        return jnp.repeat(jnp.exp(heights), extent[position] // parts).reshape((-1,) + (1,) * (len(extent) - position - 1))

    factor_of = one(*cuts[0])
    for cut in cuts[1:]:
        factor_of = factor_of * one(*cut)
    return factor_of


def shared_out(own_key, own, number, rows, count, top, reach, lean):
    order = jax.random.permutation(own_key, count)
    heavy_load, usual = shares(count, rows * top, reach, lean, True), shares(count, rows * top, reach, lean, False)
    places = jnp.arange(count)

    def named(sizes, turn):
        used = int((sizes > 0).sum())
        fixed = max(1, used // 4)
        passed = fixed + (places - fixed + turn * (used - fixed)) % max(1, count - fixed)
        return jnp.zeros((count,), jnp.int32).at[order[jnp.where(places < fixed, places, passed)]].set(jnp.asarray(sizes, jnp.int32))

    sizes = jnp.where(number % 4 == 0, named(heavy_load, number // 4), named(usual, number - number // 4 - 1))
    mixed = jax.random.permutation(jax.random.fold_in(own, 3), count)
    giver, sink = mixed[0:count // 2 * 2:2], mixed[1:count // 2 * 2:2]
    slack = jnp.minimum(sizes[giver] - 1, reach - sizes[sink]) // 2
    slack = jnp.where((giver == order[0]) | (sink == order[0]) | (sizes[sink] == 0), 0, jnp.maximum(slack, 0))
    passed = jax.random.randint(jax.random.fold_in(own, 4), (count // 2,), 0, 1 << 20) % (slack + 1)
    sizes = sizes.at[giver].add(-passed).at[sink].add(passed)
    items = jnp.searchsorted(jnp.cumsum(sizes), jnp.arange(rows * top), side="right").astype(jnp.int32)
    grid = items.reshape(top, rows).T
    grid = grid[jax.random.permutation(jax.random.fold_in(own, 1), rows)]
    turn = jax.random.randint(jax.random.fold_in(own, 2), (rows, 1), 0, top)
    return jnp.take_along_axis(grid, (jnp.arange(top)[None, :] + turn) % top, axis=1)


def shares(amount, total, limit, lean, full):
    loads = [(1 << 20) // math.isqrt(standing ** lean) + 1 for standing in range(1, amount + 1)]
    largest = limit if full else min(limit, max(-(-total // amount), total * loads[0] // sum(loads)))
    least = 1 if total - largest >= amount - 1 else 0
    holding, spare = [largest] + [least] * (amount - 1), total - largest - least * (amount - 1)
    while spare > 0:
        candidates = [i for i in range(1, amount) if holding[i] < largest] or [i for i in range(1, amount) if holding[i] < limit]
        whole, left = sum([loads[i] for i in candidates]), spare
        for i in candidates:
            extra = min(limit - holding[i], max(1, left * loads[i] // whole), spare)
            holding[i] = holding[i] + extra
            spare = spare - extra
    return np.array(holding)


def scatter_about(key, extent, scale, most, cuts=(), held_as=jnp.bfloat16):
    factor_of = steps_of(key, extent, cuts, -0.22, 0.18) if cuts else 1.0
    drawn = jax.random.normal(key, extent, jnp.float32) * scale * factor_of
    return jnp.minimum(jnp.maximum(drawn, -most), most).astype(held_as)


def setup_inputs(seed: int = 0) -> dict:
    streams_of = jax.random.split(jax.random.key(seed), 8)
    a_panels = scatter_about(streams_of[0], (N_ROW * P_SIZE * BLK, N_COL * K * BLK), 1.0, 6.0, ((0, 8), (1, 16)), jnp.float32)
    b_panels = scatter_about(streams_of[1], (N_COL * K * BLK, N_COL * Q * BLK), (TICKS * K * BLK) ** -0.5, 0.1875, ((0, 8), (1, 16)), jnp.float32)
    a_occupancy = touch_ends((jax.random.randint(streams_of[2], (N_ROW * P_SIZE, N_COL * K), 0, 3) < 2).astype(jnp.int32), jax.random.fold_in(streams_of[2], 1), 0, 1)
    b_occupancy = touch_ends((jax.random.randint(streams_of[3], (N_COL * K, N_COL * Q), 0, 3) < 2).astype(jnp.int32), jax.random.fold_in(streams_of[3], 1), 0, 1)
    owner_device_keys = jax.random.split(jax.random.fold_in(streams_of[4], 1), N_ROW * N_COL * NBLK // NBLK)
    owner_device_turns = jax.random.permutation(jax.random.fold_in(streams_of[4], 3), N_ROW * N_COL * NBLK // NBLK)
    owner_device = jax.vmap(lambda own, number: shared_out(jax.random.fold_in(streams_of[4], 2), own, number, NBLK, N_ROW * N_COL, 1, CAP, 2))(owner_device_keys, owner_device_turns).reshape((N_ROW, N_COL, NBLK, 1))
    owner_block = touch_ends(jax.random.randint(streams_of[5], (N_ROW, N_COL, NBLK), 0, OWN), jax.random.fold_in(streams_of[5], 1), 0, OWN - 1).astype(jnp.int32)
    c_previous = scatter_about(streams_of[6], (N_ROW, N_COL, OWN, BLK, BLK), 1.0, 6.0, ((0, 8), (1, 16)), jnp.float32)
    return dict(a_panels=a_panels, b_panels=b_panels, a_occupancy=a_occupancy, b_occupancy=b_occupancy, owner_device=owner_device, owner_block=owner_block, c_previous=c_previous)


def reference(a_panels, b_panels, a_occupancy, b_occupancy, owner_device, owner_block, c_previous):
    a_mask = jnp.repeat(jnp.repeat(a_occupancy.astype(jnp.float32), BLK, axis=0), BLK, axis=1)
    b_mask = jnp.repeat(jnp.repeat(b_occupancy.astype(jnp.float32), BLK, axis=0), BLK, axis=1)
    a_eff = a_panels * a_mask
    b_eff = b_panels * b_mask
    a_four = a_eff.reshape(N_ROW, P_SIZE * BLK, N_COL, K * BLK).transpose(0, 2, 1, 3)
    b_four = b_eff.reshape(N_COL, K * BLK, N_COL, Q * BLK).transpose(0, 2, 1, 3)
    start = c_previous.reshape(N_ROW * N_COL * OWN, BLK, BLK)

    def one_device(total, index):
        row_i = index // N_COL
        col_j = index % N_COL
        acc = jnp.zeros((P_SIZE * BLK, Q * BLK), jnp.float32)
        for tick in range(TICKS):
            left = a_four[row_i, (col_j + tick) % N_COL]
            slot = ((row_i + col_j + tick) % N_COL) // N_ROW
            stored = (((row_i + tick) % N_ROW) * IMAGES + slot).astype(jnp.int32)
            right = b_four[stored, col_j]
            acc = acc + jnp.dot(left, right, preferred_element_type=jnp.float32, precision=lax.Precision.HIGHEST)
        pieces = acc.reshape(P_SIZE, BLK, Q, BLK).transpose(0, 2, 1, 3).reshape(NBLK, BLK, BLK)
        owners = owner_device[row_i, col_j, :, 0].astype(jnp.int32)
        targets = owner_block[row_i, col_j].astype(jnp.int32)
        places = (owners * OWN + targets).astype(jnp.int32)
        return total.at[places].add(pieces), None

    total, unused = lax.scan(one_device, start, jnp.arange(N_ROW * N_COL, dtype=jnp.int32))
    return total.reshape(N_ROW, N_COL, OWN, BLK, BLK)
```

```python
import jax
import jax.numpy as jnp
from jax import lax
from jax.experimental import pallas as pl
from jax.experimental.pallas import tpu as pltpu
from jax.sharding import PartitionSpec as P

BLK = 128
TICKS = 4
N_ROW = 8
N_COL = 16
DEVICES = N_ROW * N_COL
NBLK = 128
CHUNKS = 4
MESH = pl.DeviceIdType.MESH
VMEM_LIMIT = 64 * 1024 * 1024 - 65536


def product_kernel(
    a_ref, b_ref, a_occ, b_occ, inv, s_out,
    a_own, b_own, b_cross, b_far, a_got, b_got, a_cat, b_cat, prod, staged,
    a_send, a_recv, b_send, b_recv, x_send, x_recv, out_sem,
):
    row = lax.axis_index("row")
    col = lax.axis_index("col")
    half = row // 4
    z = row % 4
    far = (row + 4) % N_ROW
    inner = b_ref.shape[0] // 2
    part = inner // CHUNKS

    barrier = pltpu.get_barrier_semaphore()
    peers = [(half * 4 + (z + d) % 4, col) for d in (1, 2, 3)]
    peers.append((far, col))
    peers += [(row, (col + d) % N_COL) for d in (1, 2, 3, 13, 14, 15)]
    for peer in peers:
        pl.semaphore_signal(barrier, inc=1, device_id=peer, device_id_type=MESH)

    slot_own = ((row + col) % N_COL) // N_ROW
    slot_cross = ((row + 8 * (1 - half) + col) % N_COL) // N_ROW

    def mask_right(slot, into):
        def one(n, carry):
            k = n // 16
            q = n % 16
            there = b_occ[slot * 2 + k, q].astype(jnp.float32)
            at = pl.multiple_of(q * BLK, BLK)
            into[pl.ds(k * BLK, BLK), pl.ds(at, BLK)] = (
                b_ref[pl.ds(slot * inner + k * BLK, BLK), pl.ds(at, BLK)] * there
            )
            return carry

        lax.fori_loop(0, 32, one, 0)

    mask_right(slot_cross, b_cross)
    pl.semaphore_wait(barrier, len(peers))

    def cross_copy(c):
        rows = pl.ds(c * part, part)
        return pltpu.make_async_remote_copy(
            b_cross.at[rows], b_far.at[rows], x_send.at[c], x_recv.at[c],
            device_id=(far, col), device_id_type=MESH,
        )

    def ring_copy(source, t, rows):
        return pltpu.make_async_remote_copy(
            source.at[rows], b_got.at[t - 1, rows], b_send.at[t - 1], b_recv.at[t - 1],
            device_id=(half * 4 + (z + 4 - t) % 4, col), device_id_type=MESH,
        )

    def left_copy(t):
        return pltpu.make_async_remote_copy(
            a_own, a_got.at[t - 1], a_send.at[t - 1], a_recv.at[t - 1],
            device_id=(row, (col + N_COL - t) % N_COL), device_id_type=MESH,
        )

    @pl.when(z < 3)
    def _():
        for c in range(CHUNKS):
            cross_copy(c).start()

    mask_right(slot_own, b_own)
    for t in (1, 2, 3):
        @pl.when(z >= t)
        def _(t=t):
            ring_copy(b_own, t, pl.ds(0, inner)).start()

    def mask_left(n, carry):
        p = n // 2
        for k in range(2):
            there = a_occ[p, k].astype(jnp.float32)
            at = pl.ds(p * BLK, BLK)
            a_own[at, k * BLK:(k + 1) * BLK] = a_ref[at, k * BLK:(k + 1) * BLK] * there
        return carry

    lax.fori_loop(0, 16, mask_left, 0)
    for t in (1, 2, 3):
        left_copy(t).start()

    def split_left(read):
        def one(m, carry):
            at = pl.ds(m * BLK, BLK)
            value = read(at)
            high = value.astype(jnp.bfloat16)
            low = (value - high.astype(jnp.float32)).astype(jnp.bfloat16)
            a_cat[at, 0:256] = high
            a_cat[at, 256:512] = high
            a_cat[at, 512:768] = low
            return carry

        lax.fori_loop(0, 8, one, 0)

    def split_right(read):
        def one(n, carry):
            at = pl.ds(pl.multiple_of(n * BLK, BLK), BLK)
            value = read(at)
            high = value.astype(jnp.bfloat16)
            low = (value - high.astype(jnp.float32)).astype(jnp.bfloat16)
            b_cat[0:256, at] = high
            b_cat[256:512, at] = low
            b_cat[512:768, at] = high
            return carry

        lax.fori_loop(0, 16, one, 0)

    def multiply(first):
        def one(step, carry):
            n = step // 4
            m = step % 4
            columns = pl.ds(pl.multiple_of(n * 256, 256), 256)
            tile = jnp.dot(
                a_cat[pl.ds(pl.multiple_of(m * 256, 256), 256), :], b_cat[:, columns],
                preferred_element_type=jnp.float32,
            )
            for h in range(2):
                at = pl.ds((2 * n + h) * 8 + 2 * m, 2)
                block = tile[:, h * BLK:(h + 1) * BLK].reshape(2, BLK, BLK)
                prod[at] = block if first else prod[at] + block
            return carry

        lax.fori_loop(0, 32, one, 0)

    split_left(lambda at: a_own[at, :])
    split_right(lambda at: b_own[:, at])
    multiply(True)

    @pl.when(z < 3)
    def _():
        for c in range(CHUNKS):
            cross_copy(c).wait_recv()
            for t in (1, 2, 3):
                @pl.when(z < t)
                def _(t=t):
                    ring_copy(b_far, t, pl.ds(c * part, part)).start()
        for c in range(CHUNKS):
            cross_copy(c).wait_send()

    for t in (1, 2, 3):
        left_copy(t).wait_recv()
        split_left(lambda at: a_got[t - 1, at, :])
        ring_copy(b_own, t, pl.ds(0, inner)).wait_recv()
        split_right(lambda at: b_got[t - 1, :, at])
        multiply(False)

    def place(group, carry):
        for k in range(16):
            n = group * 16 + k
            staged[n] = prod[inv[n]]
        at = pl.ds(group * 16, 16)
        pltpu.make_async_copy(staged.at[at], s_out.at[at], out_sem).start()
        return carry

    lax.fori_loop(0, 16, place, 0)
    for t in (1, 2, 3):
        left_copy(t).wait_send()
        ring_copy(b_own, t, pl.ds(0, inner)).wait_send()
    pltpu.make_async_copy(staged, s_out, out_sem).wait()


def add_kernel(targets, c_ref, got_ref, out_ref):
    step = pl.program_id(0)
    count = got_ref.shape[0]

    @pl.when(step == 0)
    def _():
        out_ref[...] = c_ref[...]

    def one(k, carry):
        target = targets[step * count + k]

        @pl.when(target >= 0)
        def _():
            out_ref[target] = out_ref[target] + got_ref[k]

        return carry

    lax.fori_loop(0, count, one, 0)


def per_device(a_panels, b_panels, a_occupancy, b_occupancy, owner_device, owner_block, c_previous):
    owners = owner_device.reshape(NBLK)
    targets = owner_block.reshape(NBLK)
    number = jnp.arange(NBLK, dtype=jnp.int32)
    named = owners[:, None] == jnp.arange(DEVICES, dtype=jnp.int32)[None, :]
    packed = number * DEVICES + targets
    first = jnp.min(jnp.where(named, packed[:, None], NBLK * DEVICES), axis=0)
    last = jnp.max(jnp.where(named, packed[:, None], -1), axis=0)
    has_first = last >= 0
    has_second = last > first
    pair = jnp.stack([jnp.where(has_first, first, 0), jnp.where(has_second, last, 0)], axis=1)
    there = jnp.stack([has_first, has_second], axis=1)
    block = pair // DEVICES
    inv = ((block % 16) * 8 + block // 16).reshape(2 * DEVICES)
    send_targets = jnp.where(there, pair % DEVICES, -1)
    got_targets = lax.all_to_all(
        send_targets, ("row", "col"), split_axis=0, concat_axis=0, tiled=True
    )

    vmem = lambda shape, dtype=jnp.float32: pltpu.VMEM(shape, dtype)
    send = pl.pallas_call(
        product_kernel,
        out_shape=jax.ShapeDtypeStruct((2 * DEVICES, BLK, BLK), jnp.float32),
        in_specs=[
            pl.BlockSpec(memory_space=pltpu.VMEM),
            pl.BlockSpec(memory_space=pltpu.VMEM),
            pl.BlockSpec(memory_space=pltpu.SMEM),
            pl.BlockSpec(memory_space=pltpu.SMEM),
            pl.BlockSpec(memory_space=pltpu.SMEM),
        ],
        out_specs=pl.BlockSpec(memory_space=pl.ANY),
        scratch_shapes=[
            vmem((1024, 256)), vmem((256, 2048)), vmem((256, 2048)), vmem((256, 2048)),
            vmem((3, 1024, 256)), vmem((3, 256, 2048)),
            vmem((1024, 768), jnp.bfloat16), vmem((768, 2048), jnp.bfloat16),
            vmem((NBLK, BLK, BLK)), vmem((2 * DEVICES, BLK, BLK)),
            pltpu.SemaphoreType.DMA((3,)), pltpu.SemaphoreType.DMA((3,)),
            pltpu.SemaphoreType.DMA((3,)), pltpu.SemaphoreType.DMA((3,)),
            pltpu.SemaphoreType.DMA((CHUNKS,)), pltpu.SemaphoreType.DMA((CHUNKS,)),
            pltpu.SemaphoreType.DMA,
        ],
        compiler_params=pltpu.CompilerParams(
            collective_id=0, has_side_effects=True, vmem_limit_bytes=VMEM_LIMIT
        ),
        name="products",
    )(a_panels, b_panels, a_occupancy, b_occupancy, inv)

    got = lax.all_to_all(
        send.reshape(DEVICES, 2, BLK, BLK), ("row", "col"), split_axis=0, concat_axis=0, tiled=True
    ).reshape(2 * DEVICES, BLK, BLK)

    owned = pl.pallas_call(
        add_kernel,
        out_shape=jax.ShapeDtypeStruct((NBLK, BLK, BLK), jnp.float32),
        grid_spec=pltpu.PrefetchScalarGridSpec(
            num_scalar_prefetch=1,
            grid=(16,),
            in_specs=[
                pl.BlockSpec((NBLK, BLK, BLK), lambda i, t: (0, 0, 0)),
                pl.BlockSpec((16, BLK, BLK), lambda i, t: (i, 0, 0)),
            ],
            out_specs=pl.BlockSpec((NBLK, BLK, BLK), lambda i, t: (0, 0, 0)),
        ),
        compiler_params=pltpu.CompilerParams(vmem_limit_bytes=VMEM_LIMIT),
        name="add_blocks",
    )(got_targets.reshape(2 * DEVICES), c_previous.reshape(NBLK, BLK, BLK), got)
    return owned.reshape(c_previous.shape)


def solution(mesh):
    in_specs = (
        P("row", "col"),
        P("row", "col"),
        P("row", "col"),
        P("row", "col"),
        P("row", "col", None, None),
        P("row", "col", None),
        P("row", "col", None, None, None),
    )
    out_specs = P("row", "col", None, None, None)
    return jax.shard_map(
        per_device, mesh=mesh, in_specs=in_specs, out_specs=out_specs, check_vma=False
    )
```

```python
import jax
import jax.numpy as jnp
from jax import lax
from jax.experimental import pallas as pl
from jax.experimental.pallas import tpu as pltpu
from jax.sharding import PartitionSpec as P

BLK = 128
TICKS = 4
N_ROW = 8
N_COL = 16
DEVICES = N_ROW * N_COL
NBLK = 128
CHUNKS = 4
ROWS = (48, 40, 40)
STARTS = (0, 48, 88)
HOPS = (1, 3, 2)
MESH = pl.DeviceIdType.MESH
VMEM_LIMIT = 64 * 1024 * 1024 - 65536


def product_kernel(
    a_ref, b_ref, a_occ, b_occ, inv, s0_out, s1_out, s2_out,
    a_own, b_own, b_cross, b_far, a_got, b_got, a_cat, b_cat, prod, staged0, staged1, staged2,
    a_send, a_recv, b_send, b_recv, x_send, x_recv, out_sem,
):
    row = lax.axis_index("row")
    col = lax.axis_index("col")
    half = row // 4
    z = row % 4
    core = col % 2
    far = (row + 4) % N_ROW
    inner = b_ref.shape[0] // 2
    part = inner // CHUNKS
    partner = col + 1 - 2 * core
    across = 3 - 2 * core

    barrier = pltpu.get_barrier_semaphore()
    peers = [(half * 4 + (z + d) % 4, col) for d in (1, 2, 3)]
    peers.append((far, col))
    peers.append((row, partner))
    peers += [(row, (col + d) % N_COL) for d in (2, 14)]
    peers.append((row, (col + 13 + 6 * core) % N_COL))
    for peer in peers:
        pl.semaphore_signal(barrier, inc=1, device_id=peer, device_id_type=MESH)

    slot_own = ((row + col) % N_COL) // N_ROW
    slot_cross = ((row + 8 * (1 - half) + col) % N_COL) // N_ROW

    def mask_right(slot, into):
        def one(n, carry):
            k = n // 16
            q = n % 16
            there = b_occ[slot * 2 + k, q].astype(jnp.float32)
            at = pl.multiple_of(q * BLK, BLK)
            into[pl.ds(k * BLK, BLK), pl.ds(at, BLK)] = (
                b_ref[pl.ds(slot * inner + k * BLK, BLK), pl.ds(at, BLK)] * there
            )
            return carry

        lax.fori_loop(0, 32, one, 0)

    mask_right(slot_cross, b_cross)
    pl.semaphore_wait(barrier, len(peers))

    def cross_copy(c):
        rows = pl.ds(c * part, part)
        return pltpu.make_async_remote_copy(
            b_cross.at[rows], b_far.at[rows], x_send.at[c], x_recv.at[c],
            device_id=(far, col), device_id_type=MESH,
        )

    def ring_copy(source, t, rows):
        return pltpu.make_async_remote_copy(
            source.at[rows], b_got.at[t - 1, rows], b_send.at[t - 1], b_recv.at[t - 1],
            device_id=(half * 4 + (z + 4 - t) % 4, col), device_id_type=MESH,
        )

    def left_copy(source, to, slot, number):
        return pltpu.make_async_remote_copy(
            source, a_got.at[slot], a_send.at[number], a_recv.at[slot],
            device_id=(row, to), device_id_type=MESH,
        )

    left_next = left_copy(a_own, (col + 14) % N_COL, 1, 0)
    left_other = left_copy(a_own, (col + N_COL - across) % N_COL, across - 1, 1)
    left_pass = left_copy(a_got.at[1], partner, 2 * core, 2)

    @pl.when(z < 3)
    def _():
        for c in range(CHUNKS):
            cross_copy(c).start()

    mask_right(slot_own, b_own)
    for t in (1, 2, 3):
        @pl.when(z >= t)
        def _(t=t):
            ring_copy(b_own, t, pl.ds(0, inner)).start()

    def mask_left(n, carry):
        for k in range(2):
            there = a_occ[n, k].astype(jnp.float32)
            at = pl.ds(n * BLK, BLK)
            a_own[at, k * BLK:(k + 1) * BLK] = a_ref[at, k * BLK:(k + 1) * BLK] * there
        return carry

    lax.fori_loop(0, 8, mask_left, 0)

    def split_left(read):
        def one(m, carry):
            at = pl.ds(m * BLK, BLK)
            value = read(at)
            high = value.astype(jnp.bfloat16)
            low = (value - high.astype(jnp.float32)).astype(jnp.bfloat16)
            a_cat[at, 0:256] = high
            a_cat[at, 256:512] = high
            a_cat[at, 512:768] = low
            return carry

        lax.fori_loop(0, 8, one, 0)

    def split_right(read):
        def one(n, carry):
            at = pl.ds(pl.multiple_of(n * BLK, BLK), BLK)
            value = read(at)
            high = value.astype(jnp.bfloat16)
            low = (value - high.astype(jnp.float32)).astype(jnp.bfloat16)
            b_cat[0:256, at] = high
            b_cat[256:512, at] = low
            b_cat[512:768, at] = high
            return carry

        lax.fori_loop(0, 16, one, 0)

    def multiply(first):
        def one(step, carry):
            n = step // 4
            m = step % 4
            columns = pl.ds(pl.multiple_of(n * 256, 256), 256)
            tile = jnp.dot(
                a_cat[pl.ds(pl.multiple_of(m * 256, 256), 256), :], b_cat[:, columns],
                preferred_element_type=jnp.float32,
            )
            for h in range(2):
                at = pl.ds((2 * n + h) * 8 + 2 * m, 2)
                block = tile[:, h * BLK:(h + 1) * BLK].reshape(2, BLK, BLK)
                prod[at] = block if first else prod[at] + block
            return carry

        lax.fori_loop(0, 32, one, 0)

    split_left(lambda at: a_own[at, :])
    split_right(lambda at: b_own[:, at])
    multiply(True)

    @pl.when(z < 3)
    def _():
        for c in range(CHUNKS):
            cross_copy(c).wait_recv()
            for t in (1, 2, 3):
                @pl.when(z < t)
                def _(t=t):
                    ring_copy(b_far, t, pl.ds(c * part, part)).start()

    left_other.start()
    left_next.start()
    left_next.wait_recv()
    left_pass.start()

    for t in (1, 2, 3):
        if t != 2:
            left_copy(a_own, partner, t - 1, 0).wait_recv()
        split_left(lambda at: a_got[t - 1, at, :])
        ring_copy(b_own, t, pl.ds(0, inner)).wait_recv()
        split_right(lambda at: b_got[t - 1, :, at])
        multiply(False)

    order = lambda u, v, w: (u * 4 + v) * 4 + w
    for g, (staged, out) in enumerate(((staged0, s0_out), (staged1, s1_out), (staged2, s2_out))):
        rows = pl.ds(STARTS[g], ROWS[g])

        def place(group, carry):
            u, v = group // 4, group % 4
            for w in range(4):
                chip = (order(u, v, w), order(w, u, v), order(v, w, u))[g]
                for k in range(4):
                    staged[u, v, w, k // 2, k % 2] = prod[inv[chip * 4 + k], rows]
            pltpu.make_async_copy(staged.at[u, v], out.at[u, v], out_sem.at[g]).start()
            return carry

        lax.fori_loop(0, 16, place, 0)

    @pl.when(z < 3)
    def _():
        for c in range(CHUNKS):
            cross_copy(c).wait_send()

    left_next.wait_send()
    left_other.wait_send()
    left_pass.wait_send()
    for t in (1, 2, 3):
        ring_copy(b_own, t, pl.ds(0, inner)).wait_send()
    for g, (staged, out) in enumerate(((staged0, s0_out), (staged1, s1_out), (staged2, s2_out))):
        pltpu.make_async_copy(staged, out, out_sem.at[g]).wait()


def exchange_kernel(*refs):
    s, r3, r1, r2 = refs[0:4], refs[4:8], refs[8:12], refs[12:16]
    (s1_send, s1_recv, s2_send, s2_recv, s3_send, s3_recv, c_send, c_recv, own_sem) = refs[16:]
    routes = range(4)
    row = lax.axis_index("row")
    col = lax.axis_index("col")
    core = col % 2
    at = (col // 4, (row // 4) * 2 + (col // 2) % 2, row % 4)

    def device(place, c):
        x, y, z = place
        return ((y // 2) * 4 + z, x * 4 + (y % 2) * 2 + c)

    def moved(dim, value):
        return tuple(value if i == dim else at[i] for i in range(3))

    barrier = pltpu.get_barrier_semaphore()
    peers = [device(at, 1 - core)]
    for dim in range(3):
        for hop in HOPS:
            for c in (core, 1 - core):
                peers.append(device(moved(dim, (at[dim] + hop) % 4), c))
    for peer in peers:
        pl.semaphore_signal(barrier, inc=1, device_id=peer, device_id_type=MESH)
    pl.semaphore_wait(barrier, len(peers))

    def dims(g):
        return g % 3, (g + 1) % 3, (g + 2) % 3

    def copy1(g, k):
        d1 = dims(g)[0]
        a = (at[d1] + HOPS[k]) % 4
        return pltpu.make_async_remote_copy(
            s[g].at[a], r1[g].at[at[d1]], s1_send.at[g], s1_recv.at[g, k],
            device_id=device(moved(d1, a), core), device_id_type=MESH,
        )

    def source1(g, k):
        return (at[dims(g)[0]] + 4 - HOPS[k]) % 4

    def copy2(g, j, k, src, a):
        d2 = dims(g)[1]
        b = (at[d2] + HOPS[j]) % 4
        return pltpu.make_async_remote_copy(
            src.at[a, b], r2[g].at[at[d2], a], s2_send.at[g], s2_recv.at[g, j, k],
            device_id=device(moved(d2, b), core), device_id_type=MESH,
        )

    def send3(g, src, b, a):
        d3 = dims(g)[2]
        into = r3[g].at[at[d3], core, b, a]
        for hop in HOPS:
            e = (at[d3] + hop) % 4
            for f in (core, 1 - core):
                pltpu.make_async_remote_copy(
                    src.at[e, f], into, s3_send.at[g], s3_recv.at[g],
                    device_id=device(moved(d3, e), f), device_id_type=MESH,
                ).start()
        pltpu.make_async_remote_copy(
            src.at[at[d3], 1 - core], into, c_send.at[g], c_recv.at[g],
            device_id=device(at, 1 - core), device_id_type=MESH,
        ).start()
        pltpu.make_async_copy(src.at[at[d3], core], into, own_sem.at[g]).start()

    def forward(g, k):
        a = at[dims(g)[0]] if k == 3 else source1(g, k)
        src = s[g] if k == 3 else r1[g]
        for j in range(3):
            copy2(g, j, k, src, a).start()
        b = at[dims(g)[1]]
        send3(g, src.at[a, b], b, a)

    def arrive2(g, k):
        a = at[dims(g)[0]] if k == 3 else source1(g, k)
        for j in range(3):
            b = (at[dims(g)[1]] + 4 - HOPS[j]) % 4
            copy2(g, j, k, s[g], a).wait_recv()
            send3(g, r2[g].at[b, a], b, a)

    for k in range(3):
        for g in routes:
            copy1(g, k).start()
    for g in routes:
        forward(g, 3)
    before = 3
    for k in range(3):
        for g in routes:
            copy1(g, k).wait_recv()
            forward(g, k)
        for g in routes:
            arrive2(g, before)
        before = k
    for g in routes:
        arrive2(g, before)
    for g in routes:
        most = r3[g].at[pl.ds(0, 3)]
        one = r3[g].at[0, 0]
        for sem in (s3_recv, s1_send, s2_send, s3_send):
            pltpu.make_async_copy(most, most, sem.at[g]).wait()
        for sem in (c_recv, c_send, own_sem):
            pltpu.make_async_copy(one, one, sem.at[g]).wait()


def add_kernel(targets, c_ref, got0, got1, got2, out_ref):
    step = pl.program_id(0)
    d3, c = step // 2, step % 2

    @pl.when(step == 0)
    def _():
        out_ref[...] = c_ref[...]

    for g, got in enumerate((got0, got1, got2)):
        rows = pl.ds(STARTS[g], ROWS[g])

        def one(n, carry):
            d2, d1, k = n // 8, (n // 2) % 4, n % 2
            x, y, z = ((d1, d2, d3), (d3, d1, d2), (d2, d3, d1))[g]
            target = targets[((z * 2 + c) * 4 + y) * 4 + x, k]

            @pl.when(target >= 0)
            def _():
                out_ref[target, rows] = out_ref[target, rows] + got[0, 0, d2, d1, k]

            return carry

        lax.fori_loop(0, 32, one, 0)


def per_device(a_panels, b_panels, a_occupancy, b_occupancy, owner_device, owner_block, c_previous):
    owners = owner_device.reshape(NBLK)
    targets = owner_block.reshape(NBLK)
    o_row, o_col = owners // N_COL, owners % N_COL
    o_y = (o_row // 4) * 2 + (o_col // 2) % 2
    places = ((o_col // 4 * 4 + o_y) * 4 + o_row % 4) * 2 + o_col % 2
    number = jnp.arange(NBLK, dtype=jnp.int32)
    named = places[:, None] == jnp.arange(DEVICES, dtype=jnp.int32)[None, :]
    packed = number * DEVICES + targets
    first = jnp.min(jnp.where(named, packed[:, None], NBLK * DEVICES), axis=0)
    last = jnp.max(jnp.where(named, packed[:, None], -1), axis=0)
    has_first = last >= 0
    has_second = last > first
    pair = jnp.stack([jnp.where(has_first, first, 0), jnp.where(has_second, last, 0)], axis=1)
    there = jnp.stack([has_first, has_second], axis=1)
    block = pair // DEVICES
    inv = ((block % 16) * 8 + block // 16).reshape(2 * DEVICES)
    send_targets = jnp.pad(
        jnp.where(there, pair % DEVICES, -1), ((0, 0), (0, BLK - 2)), constant_values=-1
    ).reshape(4, 4, 4, 2, 1, BLK)

    vmem = lambda shape, dtype=jnp.float32: pltpu.VMEM(shape, dtype)
    dma = lambda *shape: pltpu.SemaphoreType.DMA(shape)
    anywhere = pl.BlockSpec(memory_space=pl.ANY)
    blocks = lambda lead: [jax.ShapeDtypeStruct(lead + (2, r, BLK), jnp.float32) for r in ROWS]
    sent = pl.pallas_call(
        product_kernel,
        out_shape=blocks((4, 4, 4, 2)),
        in_specs=[
            pl.BlockSpec(memory_space=pltpu.VMEM),
            pl.BlockSpec(memory_space=pltpu.VMEM),
            pl.BlockSpec(memory_space=pltpu.SMEM),
            pl.BlockSpec(memory_space=pltpu.SMEM),
            pl.BlockSpec(memory_space=pltpu.SMEM),
        ],
        out_specs=[anywhere] * 3,
        scratch_shapes=[
            vmem((1024, 256)), vmem((256, 2048)), vmem((256, 2048)), vmem((256, 2048)),
            vmem((3, 1024, 256)), vmem((3, 256, 2048)),
            vmem((1024, 768), jnp.bfloat16), vmem((768, 2048), jnp.bfloat16),
            vmem((NBLK, BLK, BLK)),
            *[vmem((4, 4, 4, 2, 2, r, BLK)) for r in ROWS],
            dma(3), dma(3), dma(3), dma(3), dma(CHUNKS), dma(CHUNKS), dma(3),
        ],
        compiler_params=pltpu.CompilerParams(
            collective_id=0, has_side_effects=True, vmem_limit_bytes=VMEM_LIMIT
        ),
        name="products",
    )(a_panels, b_panels, a_occupancy, b_occupancy, inv)

    index = lambda lead: [jax.ShapeDtypeStruct(lead + (1, BLK), jnp.int32)]
    got = pl.pallas_call(
        exchange_kernel,
        out_shape=(
            blocks((4, 2, 4, 4)) + index((4, 2, 4, 4))
            + blocks((4, 4, 4, 2)) + index((4, 4, 4, 2))
            + blocks((4, 4, 4, 2)) + index((4, 4, 4, 2))
        ),
        in_specs=[anywhere] * 4,
        out_specs=[anywhere] * 12,
        scratch_shapes=[
            dma(4), dma(4, 3), dma(4), dma(4, 3, 4), dma(4), dma(4), dma(4), dma(4), dma(4),
        ],
        compiler_params=pltpu.CompilerParams(collective_id=1, has_side_effects=True),
        name="exchange",
    )(*sent, send_targets)

    owned = pl.pallas_call(
        add_kernel,
        out_shape=jax.ShapeDtypeStruct((NBLK, BLK, BLK), jnp.float32),
        grid_spec=pltpu.PrefetchScalarGridSpec(
            num_scalar_prefetch=1,
            grid=(8,),
            in_specs=[pl.BlockSpec((NBLK, BLK, BLK), lambda i, t: (0, 0, 0))] + [
                pl.BlockSpec((1, 1, 4, 4, 2, r, BLK), lambda i, t: (i // 2, i % 2, 0, 0, 0, 0, 0))
                for r in ROWS
            ],
            out_specs=pl.BlockSpec((NBLK, BLK, BLK), lambda i, t: (0, 0, 0)),
        ),
        compiler_params=pltpu.CompilerParams(vmem_limit_bytes=VMEM_LIMIT),
        name="add_blocks",
    )(got[3].reshape(DEVICES, BLK), c_previous.reshape(NBLK, BLK, BLK), *got[:3])
    return owned.reshape(c_previous.shape)


def solution(mesh):
    in_specs = (
        P("row", "col"),
        P("row", "col"),
        P("row", "col"),
        P("row", "col"),
        P("row", "col", None, None),
        P("row", "col", None),
        P("row", "col", None, None, None),
    )
    out_specs = P("row", "col", None, None, None)
    return jax.shard_map(
        per_device, mesh=mesh, in_specs=in_specs, out_specs=out_specs, check_vma=False
    )
```
